512 devices in a mesh: row: 32 (over z, core), col: 16 (over y, x).
Axes of the slice: x: 4, y: 4, z: 16, core: 2. Of those that a mesh axis runs over, the one named last changes fastest.
Arguments:
- amplitudes: bfloat16 [16384, 16384], P('row', 'col'), may hold values from -6 to 6
- integrals: bfloat16 [16384, 4096], P('col', 'row'), may hold values from -0.09375 to 0.09375
- amp_occupancy: int32 [128, 128], P('row', 'col'), may hold values 0 or 1
- int_occupancy: int32 [128, 32], P('col', 'row'), may hold values 0 or 1
- owner_map: int32 [32], replicated, may hold values from 0 to 31, each once
Outputs:
- residual: bfloat16 [16384, 4096], P('row', 'col')
The draws below stay inside these ranges and needn't reach their ends.
Inputs may be any that keep to these rules, and one draw needn't show every extreme that they name: `owner_map`: each tile number appears once.
All inputs are finite; a program needn't handle non-finite values. No bound on the sum of `amp_occupancy` or of `int_occupancy` on one device may be relied on, other than what follows from the above.
Results may differ from the reference program's by a relative error of at most 0.014.
Values may be sent and summed in bfloat16 or wider, within the bound.
No kernel may reach another device: no remote copies, remote signals or barrier semaphores. Data moves between devices by JAX's collectives and lax.ppermute only.
A program may use at most 64 MiB of HBM per device.

```python
import jax
import jax.numpy as jnp
from jax import lax

TILE = 128
KD = 1024
NJ = 4096
ROWS_ALL = 16384
K_ALL = 16384
NT = 32


def plant(result, stream_key, low, high):
    place = [jax.random.randint(jax.random.fold_in(stream_key, axis), (), 0, length) for axis, length in enumerate(result.shape)]
    widest = result.shape.index(max(result.shape))
    beside = place[:widest] + [(place[widest] + 1) % result.shape[widest]] + place[widest + 1:]
    return result.at[tuple(place)].set(low).at[tuple(beside)].set(high)


def spiked(entries, stream_key, source, target, blocks, factor):
    def block_of(axis_at):
        return (jnp.arange(entries.shape[axis_at]) // (entries.shape[axis_at] // blocks)).reshape((-1,) + (1,) * (entries.ndim - 1 - axis_at))

    one_side = jax.random.permutation(stream_key, blocks)[block_of(target)]
    second = (block_of(target) + blocks // 2) % blocks
    return jnp.where((block_of(source) == one_side) | (block_of(source) == second), factor * entries, entries)


def level_of(own_key, dims, split, low, top_value):
    loudness = 1.0
    for position, parts in split:
        steps = jax.random.uniform(jax.random.fold_in(jax.random.fold_in(own_key, 6), position), (parts,), jnp.float32, low / len(split), top_value / len(split))
        loudness = loudness * jnp.repeat(jnp.exp(steps), dims[position] // parts).reshape((-1,) + (1,) * (len(dims) - 1 - position))
    return loudness


def noise(key, extent, width, most, pieces=(), kind=jnp.bfloat16):
    array = jax.random.normal(key, extent, jnp.float32) * width
    if len(pieces) > 0:
        array = level_of(key, extent, pieces, -0.22, 0.18) * array
    return jnp.clip(array, min=-most, max=most).astype(kind)


def bell_draw_with(key, extent, spread, reach, pieces, heavy, kind=jnp.bfloat16):
    array = spread * jax.random.normal(key, extent, jnp.float32)
    if pieces:
        array = array * level_of(key, extent, pieces, -0.22, 0.18)
    return jnp.clip(spiked(array, jax.random.fold_in(key, 3), *heavy), -reach, reach).astype(kind)


def setup_inputs(seed: int = 0) -> dict:
    key_of = jax.random.split(jax.random.key(seed), 6)
    amplitudes = noise(key_of[0], (ROWS_ALL, K_ALL), 1.0, 6.0, ((0, 32), (1, 16)))
    integrals = bell_draw_with(key_of[1], (K_ALL, NJ), K_ALL ** -0.5, 0.09375, ((0, 16), (1, 32)), (0, 1, 32, 2.75))
    amp_occupancy = plant((jax.random.randint(key_of[2], (ROWS_ALL // TILE, K_ALL // TILE), 0, 3) < 2).astype(jnp.int32), jax.random.fold_in(key_of[2], 1), 0, 1)
    int_occupancy = plant((jax.random.randint(key_of[3], (K_ALL // TILE, NT), 0, 3) < 2).astype(jnp.int32), jax.random.fold_in(key_of[3], 1), 0, 1)
    owner_map = jax.random.permutation(key_of[4], NT).astype(jnp.int32)
    return dict(amplitudes=amplitudes, integrals=integrals, amp_occupancy=amp_occupancy, int_occupancy=int_occupancy, owner_map=owner_map)


def mask_tiles(matrix, occupancy):
    nrow, ncolumn = matrix.shape
    blocks = matrix.reshape(nrow // TILE, TILE, ncolumn // TILE, TILE)
    return (blocks * occupancy[:, None, :, None].astype(jnp.bfloat16)).reshape(nrow, ncolumn)


def reference(amplitudes, integrals, amp_occupancy, int_occupancy, owner_map):
    masked_amp = mask_tiles(amplitudes, amp_occupancy)
    masked_int = mask_tiles(integrals, int_occupancy)
    kall = masked_int.shape[0]
    ordered = masked_int.reshape(kall, NT, TILE)[:, owner_map, :].reshape(kall, NJ)
    nblock = kall // KD

    def accumulate(total, index):
        start = (index * KD).astype(jnp.int32)
        left = lax.dynamic_slice_in_dim(masked_amp, start, KD, 1)
        right = lax.dynamic_slice_in_dim(ordered, start, KD, 0)
        part = jnp.dot(left, right, preferred_element_type=jnp.float32).astype(jnp.bfloat16)
        part = lax.optimization_barrier(part)
        return total + part.astype(jnp.float32), None

    start_total = jnp.zeros((masked_amp.shape[0], NJ), jnp.float32)
    total, unused = lax.scan(accumulate, start_total, jnp.arange(nblock, dtype=jnp.int32))
    return total.astype(jnp.bfloat16)
```

```python
import jax
import jax.numpy as jnp
from jax import lax
from jax.sharding import Mesh, PartitionSpec as P

TILE = 128


def mask_tiles(matrix, occupancy):
    nrow, ncolumn = matrix.shape
    blocks = matrix.reshape(nrow // TILE, TILE, ncolumn // TILE, TILE)
    return (blocks * occupancy[:, None, :, None].astype(jnp.bfloat16)).reshape(nrow, ncolumn)


def ring_pairs(nz, first):
    pairs = []
    for z in range(nz):
        pairs.append((2 * z, 2 * ((z + 1) % nz)))
        pairs.append((2 * z + 1, 2 * (z if first else (z - 1) % nz) + 1))
    return pairs


def make(nz, ncol):
    row = ("z", "core")
    swap = [(r, r ^ 1) for r in range(2 * nz)]
    nslot = nz // 2
    per_chunk = 2

    def on_device(amplitudes, integrals, amp_occupancy, int_occupancy, owner_map):
        z = lax.axis_index("z")
        core = lax.axis_index("core")
        own_tile = mask_tiles(integrals, int_occupancy)
        other_tile = lax.ppermute(own_tile, row, swap)
        own_amp = mask_tiles(amplitudes, amp_occupancy)
        other_amp = lax.ppermute(own_amp, row, swap)
        nrow = own_amp.shape[0]
        amp = jnp.concatenate(
            [jnp.where(core == 0, own_amp, other_amp), jnp.where(core == 0, other_amp, own_amp)], 0
        )
        part = nrow // ncol
        current = [own_tile, other_tile]
        sums = []
        tiles = []
        for slot in range(1, nslot + 1):
            current = [lax.ppermute(c, row, ring_pairs(nz, slot == 1)) for c in current]
            tiles += current
            if slot % per_chunk == 0:
                right = jnp.concatenate(tiles, 1)
                tiles = []
                product = jnp.dot(amp, right, preferred_element_type=jnp.float32).astype(jnp.bfloat16)
                width = product.shape[1]
                product = product.reshape(2 * ncol, part, width)
                moved = lax.all_to_all(product, ("core", "col"), 0, 0, tiled=True)
                total = jnp.sum(moved.reshape(2, ncol, part, width).astype(jnp.float32), 1).astype(jnp.bfloat16)
                sums.append(total)
        done = jnp.concatenate(sums, 2).reshape(2, part, 2 * nslot, TILE)
        done = done.transpose(0, 2, 1, 3).reshape(4 * nslot, part, TILE)
        chip = owner_map // 2
        parity = owner_map % 2
        behind = (z - chip) % nz
        upward = (behind >= 1) & (behind <= nslot)
        side = jnp.where(upward, 0, 1)
        slot_of = jnp.where(upward, behind - 1, (chip - z) % nz)
        place = side * (2 * nslot) + slot_of * 2 + (parity ^ side)
        picked = done[place].reshape(ncol, 2, part, TILE).transpose(0, 2, 1, 3).reshape(ncol, part, 2 * TILE)
        final = lax.all_to_all(picked, "col", 0, 0, tiled=True)
        return final.reshape(nrow, 2 * TILE)

    return on_device


def solution(mesh):
    nz = mesh.shape["row"] // 2
    ncol = mesh.shape["col"]
    fine = Mesh(mesh.devices.reshape(nz, 2, ncol), ("z", "core", "col"))
    split = ("z", "core")
    placed = (P(split, "col"), P("col", split), P(split, "col"), P("col", split), P())
    return jax.shard_map(
        make(nz, ncol), mesh=fine, in_specs=placed, out_specs=P(split, "col"), check_vma=False
    )
```

```python
import jax
import jax.numpy as jnp
from jax import lax
from jax.sharding import Mesh, PartitionSpec as P


TILE = 128


def mask_tiles(matrix, occupancy):
    nrow, ncolumn = matrix.shape
    blocks = matrix.reshape(nrow // TILE, TILE, ncolumn // TILE, TILE)
    return (blocks * occupancy[:, None, :, None].astype(jnp.bfloat16)).reshape(nrow, ncolumn)


def ring_pairs(nz):
    up = [(2 * z, 2 * ((z + 1) % nz)) for z in range(nz)]
    down = [(2 * z + 1, 2 * ((z - 1) % nz) + 1) for z in range(nz)]
    return up + down


def first_pairs(nz, stream):
    if stream == 0:
        return [(2 * z, 2 * ((z + 1) % nz)) for z in range(nz)] + [(2 * z + 1, 2 * z + 1) for z in range(nz)]
    return [(2 * z + 1, 2 * ((z + 1) % nz)) for z in range(nz)] + [(2 * z, 2 * z + 1) for z in range(nz)]


def chunks_of(nslot):
    return (nslot // 4,) * 4


def make(nz, ncol):
    row = ("z", "core")
    swap = [(r, r ^ 1) for r in range(2 * nz)]
    nslot = nz // 2
    sizes = chunks_of(nslot)
    ends = [sum(sizes[: i + 1]) for i in range(len(sizes))]

    def on_device(amplitudes, integrals, amp_occupancy, int_occupancy, owner_map):
        z = lax.axis_index("z")
        core = lax.axis_index("core")
        own_tile = mask_tiles(integrals, int_occupancy)
        current = [own_tile, own_tile]
        sums = []
        tiles = []
        amp = None
        for slot in range(1, nslot + 1):
            for stream in (0, 1):
                pairs = first_pairs(nz, stream) if slot == 1 else ring_pairs(nz)
                current[stream] = lax.ppermute(current[stream], row, pairs)
            tiles += current
            if slot == 1:
                own_amp = mask_tiles(amplitudes, amp_occupancy)
                other_amp = lax.ppermute(own_amp, row, swap)
                amp = jnp.concatenate(
                    [jnp.where(core == 0, own_amp, other_amp), jnp.where(core == 0, other_amp, own_amp)], 0
                )
                nrow = own_amp.shape[0]
                part = nrow // ncol
            if slot in ends:
                right = jnp.concatenate(tiles, 1)
                product = jnp.dot(amp, right, preferred_element_type=jnp.float32).astype(jnp.bfloat16)
                tiles = []
                width = product.shape[1]
                product = product.reshape(2 * ncol, part, width)
                moved = lax.all_to_all(product, ("core", "col"), 0, 0, tiled=True)
                total = jnp.sum(moved.reshape(2, ncol, part, width).astype(jnp.float32), 1)
                sums.append(total.astype(jnp.bfloat16))
        done = jnp.concatenate(sums, 2).reshape(2, part, 2 * nslot, TILE)
        done = done.transpose(0, 2, 1, 3).reshape(4 * nslot, part, TILE)
        chip = owner_map // 2
        parity = owner_map % 2
        behind = (z - chip) % nz
        upward = (behind >= 1) & (behind <= nslot)
        side = jnp.where(upward, 0, 1)
        slot_of = jnp.where(upward, behind - 1, (chip - z) % nz)
        place = side * (2 * nslot) + slot_of * 2 + (parity ^ side)
        picked = done[place].reshape(ncol, 2, part, TILE).transpose(0, 2, 1, 3).reshape(ncol, part, 2 * TILE)
        final = lax.all_to_all(picked, "col", 0, 0, tiled=True)
        return final.reshape(nrow, 2 * TILE)

    return on_device


def solution(mesh):
    nz = mesh.shape["row"] // 2
    ncol = mesh.shape["col"]
    fine = Mesh(mesh.devices.reshape(nz, 2, ncol), ("z", "core", "col"))
    split = ("z", "core")
    placed = (P(split, "col"), P("col", split), P(split, "col"), P("col", split), P())
    return jax.shard_map(
        make(nz, ncol), mesh=fine, in_specs=placed, out_specs=P(split, "col"), check_vma=False
    )
```

```python
import jax
import jax.numpy as jnp
from jax import lax
from jax.sharding import Mesh, PartitionSpec as P


TILE = 128


def mask_tiles(matrix, occupancy):
    nrow, ncolumn = matrix.shape
    blocks = matrix.reshape(nrow // TILE, TILE, ncolumn // TILE, TILE)
    return (blocks * occupancy[:, None, :, None].astype(jnp.bfloat16)).reshape(nrow, ncolumn)


def rank(nz, ncol, z, core, col):
    return ((z % nz) * 2 + core) * ncol + col


def ring_pairs(nz, ncol):
    pairs = []
    for z in range(nz):
        for col in range(ncol):
            pairs.append((rank(nz, ncol, z, 0, col), rank(nz, ncol, z + 1, 0, col)))
            pairs.append((rank(nz, ncol, z, 1, col), rank(nz, ncol, z - 1, 1, col)))
    return pairs


def first_pairs(nz, ncol, stream):
    pairs = []
    for z in range(nz):
        for col in range(ncol):
            even = col & ~1
            for core in (0, 1):
                source = rank(nz, ncol, z, col & 1, even | (core ^ stream))
                target = rank(nz, ncol, z + 1 if core == 0 else z, core, col)
                pairs.append((source, target))
    return pairs


def swap_pairs(nz, ncol, core, col):
    return [
        (rank(nz, ncol, z, c, x), rank(nz, ncol, z, c ^ core, x ^ col))
        for z in range(nz) for c in (0, 1) for x in range(ncol)
    ]


def chunks_of(nslot):
    last = 3 * nslot // 8
    return (nslot - last, last)


def make(nz, ncol):
    every = ("z", "core", "col")
    nslot = nz // 2
    sizes = chunks_of(nslot)
    ends = [sum(sizes[: i + 1]) for i in range(len(sizes))]

    def on_device(amplitudes, integrals, amp_occupancy, int_occupancy, owner_map):
        z = lax.axis_index("z")
        core = lax.axis_index("core")
        odd = lax.axis_index("col") % 2
        own_tile = mask_tiles(integrals, int_occupancy)
        nrow, kloc = amplitudes.shape
        part = nrow // ncol
        current = [own_tile, own_tile]
        sums = []
        tiles = [[], []]
        for slot in range(1, nslot + 1):
            for stream in (0, 1):
                pairs = first_pairs(nz, ncol, stream) if slot == 1 else ring_pairs(nz, ncol)
                current[stream] = lax.ppermute(current[stream], every, pairs)
                tiles[stream].append(current[stream])
            if slot == 1:
                own = mask_tiles(amplitudes, amp_occupancy)
                beside = lax.ppermute(own, every, swap_pairs(nz, ncol, 0, 1))
                own_other = lax.ppermute(own, every, swap_pairs(nz, ncol, 1, 0))
                beside_other = lax.ppermute(beside, every, swap_pairs(nz, ncol, 1, 0))
                first = (odd ^ core) * kloc
                second = kloc - first
                mine = core * nrow
                theirs = nrow - mine
                amp = jnp.zeros((2 * nrow, 2 * kloc), jnp.bfloat16)
                amp = lax.dynamic_update_slice(amp, own, (mine, first))
                amp = lax.dynamic_update_slice(amp, own_other, (theirs, first))
                amp = lax.dynamic_update_slice(amp, beside, (mine, second))
                amp = lax.dynamic_update_slice(amp, beside_other, (theirs, second))
            if slot in ends:
                right = jnp.concatenate([jnp.concatenate(t, 1) for t in tiles], 0)
                product = jnp.dot(amp, right, preferred_element_type=jnp.float32).astype(jnp.bfloat16)
                tiles = [[], []]
                width = product.shape[1]
                product = product.reshape(2 * ncol, part, width)
                moved = lax.all_to_all(product, ("core", "col"), 0, 0, tiled=True)
                moved = moved.reshape(2, ncol // 2, 2, part, width)
                total = jnp.sum(moved.astype(jnp.float32), 1)
                sums.append(total.astype(jnp.bfloat16))
        done = jnp.concatenate(sums, 3).reshape(4, part, nslot, TILE)
        done = done.transpose(0, 2, 1, 3).reshape(4 * nslot, part, TILE)
        chip = owner_map // 2
        parity = owner_map % 2
        behind = (z - chip) % nz
        upward = (behind >= 1) & (behind <= nslot)
        side = jnp.where(upward, 0, 2)
        slot_of = jnp.where(upward, behind - 1, (chip - z) % nz)
        place = (side + parity) * nslot + slot_of
        picked = done[place].reshape(ncol, 2, part, TILE).transpose(0, 2, 1, 3).reshape(ncol, part, 2 * TILE)
        final = lax.all_to_all(picked, "col", 0, 0, tiled=True)
        return final.reshape(nrow, 2 * TILE)

    return on_device


def solution(mesh):
    nz = mesh.shape["row"] // 2
    ncol = mesh.shape["col"]
    fine = Mesh(mesh.devices.reshape(nz, 2, ncol), ("z", "core", "col"))
    split = ("z", "core")
    placed = (P(split, "col"), P("col", split), P(split, "col"), P("col", split), P())
    return jax.shard_map(
        make(nz, ncol), mesh=fine, in_specs=placed, out_specs=P(split, "col"), check_vma=False
    )
```

```python
import jax
import jax.numpy as jnp
from jax import lax
from jax.experimental import pallas as pl
from jax.experimental.pallas import tpu as pltpu
from jax.sharding import Mesh, PartitionSpec as P


TILE = 128


def mask_tiles(matrix, occupancy):
    nrow, ncolumn = matrix.shape
    blocks = matrix.reshape(nrow // TILE, TILE, ncolumn // TILE, TILE)
    return (blocks * occupancy[:, None, :, None].astype(jnp.bfloat16)).reshape(nrow, ncolumn)


def rank(nz, ncol, z, core, col):
    return ((z % nz) * 2 + core) * ncol + col


def ring_pairs(nz, ncol):
    pairs = []
    for z in range(nz):
        for col in range(ncol):
            pairs.append((rank(nz, ncol, z, 0, col), rank(nz, ncol, z + 1, 0, col)))
            pairs.append((rank(nz, ncol, z, 1, col), rank(nz, ncol, z - 1, 1, col)))
    return pairs


def first_pairs(nz, ncol, stream):
    pairs = []
    for z in range(nz):
        for col in range(ncol):
            even = col & ~1
            for core in (0, 1):
                source = rank(nz, ncol, z, col & 1, even | (core ^ stream))
                target = rank(nz, ncol, z + 1 if core == 0 else z, core, col)
                pairs.append((source, target))
    return pairs


def swap_pairs(nz, ncol, core, col):
    return [
        (rank(nz, ncol, z, c, x), rank(nz, ncol, z, c ^ core, x ^ col))
        for z in range(nz) for c in (0, 1) for x in range(ncol)
    ]


def chunks_of(nslot):
    last = 3 * nslot // 8
    return (nslot - last, last)


def multiply(choice, blocks, tiles):
    nrow, kloc = blocks[0].shape
    count = len(tiles[0])
    width = count * TILE
    step = nrow // 2

    def body(choice_ref, own, beside, own_other, beside_other, *rest):
        tile_refs, out, right = rest[: 2 * count], rest[2 * count], rest[2 * count + 1]

        @pl.when(pl.program_id(0) == 0)
        def _():
            for i in range(2 * count):
                right[i // count, :, (i % count) * TILE : (i % count + 1) * TILE] = tile_refs[i][...]

        near = jnp.concatenate([own[...], own_other[...]], 0)
        far = jnp.concatenate([beside[...], beside_other[...]], 0)
        stream, core = choice_ref[0], choice_ref[1]
        for start in range(0, width, 2 * TILE):
            cols = slice(start, min(start + 2 * TILE, width))
            total = jnp.dot(near, right[stream, :, cols], preferred_element_type=jnp.float32)
            total += jnp.dot(far, right[1 - stream, :, cols], preferred_element_type=jnp.float32)
            total = total.astype(jnp.bfloat16)
            out[core, :, cols] = total[:step]
            out[1 - core, :, cols] = total[step:]

    left = pl.BlockSpec((step, kloc), lambda m: (m, 0))
    whole = pl.BlockSpec((kloc, TILE), lambda m: (0, 0))
    return pl.pallas_call(
        body,
        grid=(nrow // step,),
        in_specs=[pl.BlockSpec(memory_space=pltpu.SMEM)] + [left] * 4 + [whole] * (2 * count),
        out_specs=pl.BlockSpec((2, step, width), lambda m: (0, m, 0)),
        out_shape=jax.ShapeDtypeStruct((2, nrow, width), jnp.bfloat16),
        scratch_shapes=[pltpu.VMEM((2, kloc, width), jnp.bfloat16)],
        name="multiply",
    )(choice, *blocks, *tiles[0], *tiles[1])


def make(nz, ncol):
    every = ("z", "core", "col")
    nslot = nz // 2
    sizes = chunks_of(nslot)
    ends = [sum(sizes[: i + 1]) for i in range(len(sizes))]

    def on_device(amplitudes, integrals, amp_occupancy, int_occupancy, owner_map):
        z = lax.axis_index("z")
        core = lax.axis_index("core")
        odd = lax.axis_index("col") % 2
        own_tile = mask_tiles(integrals, int_occupancy)
        nrow, _ = amplitudes.shape
        part = nrow // ncol
        current = [own_tile, own_tile]
        sums = []
        tiles = [[], []]
        for slot in range(1, nslot + 1):
            for stream in (0, 1):
                pairs = first_pairs(nz, ncol, stream) if slot == 1 else ring_pairs(nz, ncol)
                current[stream] = lax.ppermute(current[stream], every, pairs)
                tiles[stream].append(current[stream])
            if slot == 1:
                own = mask_tiles(amplitudes, amp_occupancy)
                beside = lax.ppermute(own, every, swap_pairs(nz, ncol, 0, 1))
                own_other = lax.ppermute(own, every, swap_pairs(nz, ncol, 1, 0))
                beside_other = lax.ppermute(beside, every, swap_pairs(nz, ncol, 1, 0))
                blocks = (own, beside, own_other, beside_other)
                choice = jnp.stack([odd ^ core, core]).astype(jnp.int32)
            if slot in ends:
                product = multiply(choice, blocks, tiles)
                tiles = [[], []]
                width = product.shape[-1]
                product = product.reshape(2 * ncol, part, width)
                moved = lax.all_to_all(product, ("core", "col"), 0, 0, tiled=True)
                moved = moved.reshape(2, ncol // 2, 2, part, width)
                total = jnp.sum(moved.astype(jnp.float32), 1)
                sums.append(total.astype(jnp.bfloat16))
        done = jnp.concatenate(sums, 3).reshape(4, part, nslot, TILE)
        done = done.transpose(0, 2, 1, 3).reshape(4 * nslot, part, TILE)
        chip = owner_map // 2
        parity = owner_map % 2
        behind = (z - chip) % nz
        upward = (behind >= 1) & (behind <= nslot)
        side = jnp.where(upward, 0, 2)
        slot_of = jnp.where(upward, behind - 1, (chip - z) % nz)
        place = (side + parity) * nslot + slot_of
        picked = done[place].reshape(ncol, 2, part, TILE).transpose(0, 2, 1, 3).reshape(ncol, part, 2 * TILE)
        final = lax.all_to_all(picked, "col", 0, 0, tiled=True)
        return final.reshape(nrow, 2 * TILE)

    return on_device


def solution(mesh):
    nz = mesh.shape["row"] // 2
    ncol = mesh.shape["col"]
    fine = Mesh(mesh.devices.reshape(nz, 2, ncol), ("z", "core", "col"))
    split = ("z", "core")
    placed = (P(split, "col"), P("col", split), P(split, "col"), P("col", split), P())
    return jax.shard_map(
        make(nz, ncol), mesh=fine, in_specs=placed, out_specs=P(split, "col"), check_vma=False
    )
```

```python
import jax
import jax.numpy as jnp
from jax import lax
from jax.experimental import pallas as pl
from jax.experimental.pallas import tpu as pltpu
from jax.sharding import Mesh, PartitionSpec as P


TILE = 128


def mask_tiles(matrix, occupancy):
    nrow, ncolumn = matrix.shape
    blocks = matrix.reshape(nrow // TILE, TILE, ncolumn // TILE, TILE)
    return (blocks * occupancy[:, None, :, None].astype(jnp.bfloat16)).reshape(nrow, ncolumn)


def rank(nz, ncol, z, core, col):
    return ((z % nz) * 2 + core) * ncol + col


def ring_pairs(nz, ncol):
    pairs = []
    for z in range(nz):
        for col in range(ncol):
            pairs.append((rank(nz, ncol, z, 0, col), rank(nz, ncol, z + 1, 0, col)))
            pairs.append((rank(nz, ncol, z, 1, col), rank(nz, ncol, z - 1, 1, col)))
    return pairs


def first_pairs(nz, ncol, stream):
    pairs = []
    for z in range(nz):
        for col in range(ncol):
            even = col & ~1
            for core in (0, 1):
                source = rank(nz, ncol, z, col & 1, even | (core ^ stream))
                target = rank(nz, ncol, z + 1 if core == 0 else z, core, col)
                pairs.append((source, target))
    return pairs


def swap_pairs(nz, ncol, core, col):
    return [
        (rank(nz, ncol, z, c, x), rank(nz, ncol, z, c ^ core, x ^ col))
        for z in range(nz) for c in (0, 1) for x in range(ncol)
    ]


CHUNKS = ((3, 2), (2, 1))


def calls_of():
    calls = []
    slot = 0
    for k, chunk in enumerate(CHUNKS):
        begin = 0
        for count in chunk:
            slot += count
            calls.append((slot, k, count, begin, sum(chunk)))
            begin += count
    return calls


def masked_tile(integrals, occupancy):
    def body(occ, tile, out):
        for k in range(tile.shape[0] // TILE):
            rows = slice(k * TILE, (k + 1) * TILE)
            out[rows, :] = tile[rows, :] * occ[k].astype(jnp.float32).astype(jnp.bfloat16)

    return pl.pallas_call(
        body,
        in_specs=[pl.BlockSpec(memory_space=pltpu.SMEM), pl.BlockSpec(memory_space=pltpu.VMEM)],
        out_specs=pl.BlockSpec(memory_space=pltpu.VMEM),
        out_shape=jax.ShapeDtypeStruct(integrals.shape, jnp.bfloat16),
        name="masked_tile",
    )(occupancy.reshape(-1), integrals)


def multiply(choice, blocks, tiles, start, width, previous):
    nrow, kloc = blocks[0].shape
    count = len(tiles[0])
    part = count * TILE
    step = nrow // 2
    steps = nrow // step

    def body(choice_ref, own, beside, own_other, beside_other, *rest):
        tile_refs = rest[: 2 * count]
        out, right, total, sem = rest[-4:]
        m = pl.program_id(0)
        stream, core = choice_ref[0], choice_ref[1]

        def copy_out(at, half):
            side = core if half == 0 else 1 - core
            target = out.at[side, pl.ds(at * step, step), pl.ds(start, part)]
            return pltpu.make_async_copy(total.at[at, half], target, sem.at[at, half])

        @pl.when(m == 0)
        def _():
            for i in range(2 * count):
                right[i // count, :, (i % count) * TILE : (i % count + 1) * TILE] = tile_refs[i][...]

        near = jnp.concatenate([own[...], own_other[...]], 0)
        far = jnp.concatenate([beside[...], beside_other[...]], 0)
        for first in range(0, part, 2 * TILE):
            cols = slice(first, min(first + 2 * TILE, part))
            value = jnp.dot(near, right[stream, :, cols], preferred_element_type=jnp.float32)
            value += jnp.dot(far, right[1 - stream, :, cols], preferred_element_type=jnp.float32)
            value = value.astype(jnp.bfloat16)
            total[m, 0, :, cols] = value[:step]
            total[m, 1, :, cols] = value[step:]
        for half in (0, 1):
            copy_out(m, half).start()

        @pl.when(m == steps - 1)
        def _():
            for at in range(steps):
                for half in (0, 1):
                    copy_out(at, half).wait()

    left = pl.BlockSpec((step, kloc), lambda m: (m, 0))
    whole = pl.BlockSpec((kloc, TILE), lambda m: (0, 0))
    anywhere = pl.BlockSpec(memory_space=pl.ANY)
    operands = [choice, *blocks, *tiles[0], *tiles[1]]
    specs = [pl.BlockSpec(memory_space=pltpu.SMEM)] + [left] * 4 + [whole] * (2 * count)
    aliases = {}
    if previous is not None:
        aliases = {len(operands): 0}
        operands.append(previous)
        specs.append(anywhere)
    return pl.pallas_call(
        body,
        grid=(steps,),
        in_specs=specs,
        out_specs=anywhere,
        out_shape=jax.ShapeDtypeStruct((2, nrow, width), jnp.bfloat16),
        scratch_shapes=[
            pltpu.VMEM((2, kloc, part), jnp.bfloat16),
            pltpu.VMEM((steps, 2, step, part), jnp.bfloat16),
            pltpu.SemaphoreType.DMA((steps, 2)),
        ],
        input_output_aliases=aliases,
        name="multiply",
    )(*operands)


def make(nz, ncol):
    every = ("z", "core", "col")
    nslot = nz // 2
    assert sum(map(sum, CHUNKS)) == nslot

    def on_device(amplitudes, integrals, amp_occupancy, int_occupancy, owner_map):
        z = lax.axis_index("z")
        core = lax.axis_index("core")
        odd = lax.axis_index("col") % 2
        own_tile = masked_tile(integrals, int_occupancy)
        nrow, _ = amplitudes.shape
        part = nrow // ncol
        current = [own_tile, own_tile]
        sums = []
        tiles = [[], []]
        ends = calls_of()
        call = 0
        product = None
        for slot in range(1, nslot + 1):
            for stream in (0, 1):
                pairs = first_pairs(nz, ncol, stream) if slot == 1 else ring_pairs(nz, ncol)
                current[stream] = lax.ppermute(current[stream], every, pairs)
                tiles[stream].append(current[stream])
            if slot == 1:
                own = mask_tiles(amplitudes, amp_occupancy)
                beside = lax.ppermute(own, every, swap_pairs(nz, ncol, 0, 1))
                own_other = lax.ppermute(own, every, swap_pairs(nz, ncol, 1, 0))
                beside_other = lax.ppermute(beside, every, swap_pairs(nz, ncol, 1, 0))
                blocks = (own, beside, own_other, beside_other)
                choice = jnp.stack([odd ^ core, core]).astype(jnp.int32)
            if slot == ends[call][0]:
                _, _, count, begin, width = ends[call]
                product = multiply(choice, blocks, tiles, begin * TILE, width * TILE, product)
                tiles = [[], []]
                call += 1
                if begin + count < width:
                    continue
                width = product.shape[-1]
                moved = product.reshape(2 * ncol, part, width)
                product = None
                moved = lax.all_to_all(moved, ("core", "col"), 0, 0, tiled=True)
                moved = moved.reshape(2, ncol // 2, 2, part, width)
                total = jnp.sum(moved.astype(jnp.float32), 1)
                sums.append(total.astype(jnp.bfloat16))
        done = jnp.concatenate(sums, 3).reshape(4, part, nslot, TILE)
        done = done.transpose(0, 2, 1, 3).reshape(4 * nslot, part, TILE)
        chip = owner_map // 2
        parity = owner_map % 2
        behind = (z - chip) % nz
        upward = (behind >= 1) & (behind <= nslot)
        side = jnp.where(upward, 0, 2)
        slot_of = jnp.where(upward, behind - 1, (chip - z) % nz)
        place = (side + parity) * nslot + slot_of
        picked = done[place].reshape(ncol, 2, part, TILE).transpose(0, 2, 1, 3).reshape(ncol, part, 2 * TILE)
        final = lax.all_to_all(picked, "col", 0, 0, tiled=True)
        return final.reshape(nrow, 2 * TILE)

    return on_device


def solution(mesh):
    nz = mesh.shape["row"] // 2
    ncol = mesh.shape["col"]
    fine = Mesh(mesh.devices.reshape(nz, 2, ncol), ("z", "core", "col"))
    split = ("z", "core")
    placed = (P(split, "col"), P("col", split), P(split, "col"), P("col", split), P())
    return jax.shard_map(
        make(nz, ncol), mesh=fine, in_specs=placed, out_specs=P(split, "col"), check_vma=False
    )
```

```python
import jax
import jax.numpy as jnp
from jax import lax
from jax.experimental import pallas as pl
from jax.experimental.pallas import tpu as pltpu
from jax.sharding import Mesh, PartitionSpec as P


TILE = 128
KERNEL_VMEM = 16 << 20


def mask_tiles(matrix, occupancy):
    nrow, ncolumn = matrix.shape
    blocks = matrix.reshape(nrow // TILE, TILE, ncolumn // TILE, TILE)
    return (blocks * occupancy[:, None, :, None].astype(jnp.bfloat16)).reshape(nrow, ncolumn)


def rank(nz, ncol, z, core, col):
    return ((z % nz) * 2 + core) * ncol + col


def ring_pairs(nz, ncol):
    pairs = []
    for z in range(nz):
        for col in range(ncol):
            pairs.append((rank(nz, ncol, z, 0, col), rank(nz, ncol, z + 1, 0, col)))
            pairs.append((rank(nz, ncol, z, 1, col), rank(nz, ncol, z - 1, 1, col)))
    return pairs


def first_pairs(nz, ncol, stream):
    pairs = []
    for z in range(nz):
        for col in range(ncol):
            even = col & ~1
            for core in (0, 1):
                source = rank(nz, ncol, z, col & 1, even | (core ^ stream))
                target = rank(nz, ncol, z + 1 if core == 0 else z, core, col)
                pairs.append((source, target))
    return pairs


def swap_pairs(nz, ncol, core, col):
    return [
        (rank(nz, ncol, z, c, x), rank(nz, ncol, z, c ^ core, x ^ col))
        for z in range(nz) for c in (0, 1) for x in range(ncol)
    ]


CHUNKS = ((3, 2), (2, 1))


def calls_of():
    calls = []
    slot = 0
    for k, chunk in enumerate(CHUNKS):
        begin = 0
        for count in chunk:
            slot += count
            calls.append((slot, k, count, begin, sum(chunk)))
            begin += count
    return calls


def masked_tile(integrals, occupancy):
    def body(occ, tile, out):
        for k in range(tile.shape[0] // TILE):
            rows = slice(k * TILE, (k + 1) * TILE)
            out[rows, :] = tile[rows, :] * occ[k].astype(jnp.float32).astype(jnp.bfloat16)

    return pl.pallas_call(
        body,
        in_specs=[pl.BlockSpec(memory_space=pltpu.SMEM), pl.BlockSpec(memory_space=pltpu.VMEM)],
        out_specs=pl.BlockSpec(memory_space=pltpu.VMEM),
        out_shape=pltpu.VMEM(integrals.shape, jnp.bfloat16),
        compiler_params=pltpu.CompilerParams(vmem_limit_bytes=KERNEL_VMEM),
        name="masked_tile",
    )(occupancy.reshape(-1), integrals)


def multiply(blocks, tiles, start, width, previous):
    nrow, kloc = blocks[0].shape
    count = len(tiles[0])
    part = count * TILE

    def body(own, beside, own_other, beside_other, *rest):
        tile_refs = rest[: 2 * count]
        out, right = rest[-2:]
        core = lax.axis_index("core")
        stream = (lax.axis_index("col") + core) % 2
        for i in range(2 * count):
            right[i // count, :, (i % count) * TILE : (i % count + 1) * TILE] = tile_refs[i][...]
        for side, near, far in ((core, own, beside), (1 - core, own_other, beside_other)):
            for first in range(0, part, 2 * TILE):
                last = min(first + 2 * TILE, part)
                value = jnp.dot(near[...], right[stream, :, first:last], preferred_element_type=jnp.float32)
                value += jnp.dot(far[...], right[1 - stream, :, first:last], preferred_element_type=jnp.float32)
                out[side, :, start + first : start + last] = value.astype(jnp.bfloat16)

    vmem = pl.BlockSpec(memory_space=pltpu.VMEM)
    operands = [*blocks, *tiles[0], *tiles[1]]
    aliases = {}
    if previous is not None:
        aliases = {len(operands): 0}
        operands.append(previous)
    return pl.pallas_call(
        body,
        in_specs=[vmem] * len(operands),
        out_specs=vmem,
        out_shape=pltpu.VMEM((2, nrow, width), jnp.bfloat16),
        scratch_shapes=[pltpu.VMEM((2, kloc, part), jnp.bfloat16)],
        input_output_aliases=aliases,
        compiler_params=pltpu.CompilerParams(vmem_limit_bytes=KERNEL_VMEM),
        name="multiply",
    )(*[pltpu.with_memory_space_constraint(o, pltpu.VMEM) for o in operands])


def make(nz, ncol):
    every = ("z", "core", "col")
    nslot = nz // 2
    assert sum(map(sum, CHUNKS)) == nslot

    def on_device(amplitudes, integrals, amp_occupancy, int_occupancy, owner_map):
        z = lax.axis_index("z")
        own_tile = masked_tile(integrals, int_occupancy)
        nrow, _ = amplitudes.shape
        part = nrow // ncol
        current = [own_tile, own_tile]
        sums = []
        tiles = [[], []]
        ends = calls_of()
        call = 0
        product = None
        for slot in range(1, nslot + 1):
            for stream in (0, 1):
                pairs = first_pairs(nz, ncol, stream) if slot == 1 else ring_pairs(nz, ncol)
                current[stream] = lax.ppermute(current[stream], every, pairs)
                tiles[stream].append(current[stream])
            if slot == 1:
                own = mask_tiles(amplitudes, amp_occupancy)
                beside = lax.ppermute(own, every, swap_pairs(nz, ncol, 0, 1))
                own_other = lax.ppermute(own, every, swap_pairs(nz, ncol, 1, 0))
                beside_other = lax.ppermute(beside, every, swap_pairs(nz, ncol, 1, 0))
                blocks = (own, beside, own_other, beside_other)
            if slot == ends[call][0]:
                _, _, count, begin, width = ends[call]
                product = multiply(blocks, tiles, begin * TILE, width * TILE, product)
                tiles = [[], []]
                call += 1
                if begin + count < width:
                    continue
                width = product.shape[-1]
                moved = product.reshape(2 * ncol, part, width)
                product = None
                moved = lax.all_to_all(moved, ("core", "col"), 0, 0, tiled=True)
                moved = moved.reshape(2, ncol // 2, 2, part, width)
                total = jnp.sum(moved.astype(jnp.float32), 1)
                sums.append(total.astype(jnp.bfloat16))
        done = jnp.concatenate(sums, 3).reshape(4, part, nslot, TILE)
        done = done.transpose(0, 2, 1, 3).reshape(4 * nslot, part, TILE)
        chip = owner_map // 2
        parity = owner_map % 2
        behind = (z - chip) % nz
        upward = (behind >= 1) & (behind <= nslot)
        side = jnp.where(upward, 0, 2)
        slot_of = jnp.where(upward, behind - 1, (chip - z) % nz)
        place = (side + parity) * nslot + slot_of
        picked = done[place].reshape(ncol, 2, part, TILE).transpose(0, 2, 1, 3).reshape(ncol, part, 2 * TILE)
        final = lax.all_to_all(picked, "col", 0, 0, tiled=True)
        return final.reshape(nrow, 2 * TILE)

    return on_device


def solution(mesh):
    nz = mesh.shape["row"] // 2
    ncol = mesh.shape["col"]
    fine = Mesh(mesh.devices.reshape(nz, 2, ncol), ("z", "core", "col"))
    split = ("z", "core")
    placed = (P(split, "col"), P("col", split), P(split, "col"), P("col", split), P())
    return jax.shard_map(
        make(nz, ncol), mesh=fine, in_specs=placed, out_specs=P(split, "col"), check_vma=False
    )
```

```python
import jax
import jax.numpy as jnp
from jax import lax
from jax.experimental import pallas as pl
from jax.experimental.pallas import tpu as pltpu
from jax.sharding import Mesh, PartitionSpec as P


TILE = 128
KERNEL_VMEM = 16 << 20


def mask_tiles(matrix, occupancy):
    nrow, ncolumn = matrix.shape
    blocks = matrix.reshape(nrow // TILE, TILE, ncolumn // TILE, TILE)
    return (blocks * occupancy[:, None, :, None].astype(jnp.bfloat16)).reshape(nrow, ncolumn)


def rank(nz, ncol, z, core, col):
    return ((z % nz) * 2 + core) * ncol + col


def ring_pairs(nz, ncol):
    pairs = []
    for z in range(nz):
        for col in range(ncol):
            pairs.append((rank(nz, ncol, z, 0, col), rank(nz, ncol, z + 1, 0, col)))
            pairs.append((rank(nz, ncol, z, 1, col), rank(nz, ncol, z - 1, 1, col)))
    return pairs


def first_pairs(nz, ncol, stream):
    pairs = []
    for z in range(nz):
        for col in range(ncol):
            even = col & ~1
            for core in (0, 1):
                source = rank(nz, ncol, z, col & 1, even | (core ^ stream))
                target = rank(nz, ncol, z + 1 if core == 0 else z, core, col)
                pairs.append((source, target))
    return pairs


def swap_pairs(nz, ncol, core, col):
    return [
        (rank(nz, ncol, z, c, x), rank(nz, ncol, z, c ^ core, x ^ col))
        for z in range(nz) for c in (0, 1) for x in range(ncol)
    ]


NX = 4
CALLS = (4, 2, 1, 1)


def masked_tile(integrals, occupancy):
    def body(occ, tile, out):
        for k in range(tile.shape[0] // TILE):
            rows = slice(k * TILE, (k + 1) * TILE)
            out[rows, :] = tile[rows, :] * occ[k].astype(jnp.float32).astype(jnp.bfloat16)

    return pl.pallas_call(
        body,
        in_specs=[pl.BlockSpec(memory_space=pltpu.SMEM), pl.BlockSpec(memory_space=pltpu.VMEM)],
        out_specs=pl.BlockSpec(memory_space=pltpu.VMEM),
        out_shape=pltpu.VMEM(integrals.shape, jnp.bfloat16),
        compiler_params=pltpu.CompilerParams(vmem_limit_bytes=KERNEL_VMEM),
        name="masked_tile",
    )(occupancy.reshape(-1), integrals)


def multiply(blocks, tiles):
    nrow, kloc = blocks[0].shape
    count = len(tiles[0])
    width = count * TILE
    band = nrow // 4

    def body(own, beside, own_other, beside_other, *rest):
        tile_refs = rest[: 2 * count]
        keep, give, right, both = rest[2 * count :]
        core = lax.axis_index("core")
        odd = lax.axis_index("yp")
        stream = (lax.axis_index("x") + core) % 2
        for i in range(2 * count):
            right[i // count, :, (i % count) * TILE : (i % count + 1) * TILE] = tile_refs[i][...]
        for side, near, far in ((core, own, beside), (1 - core, own_other, beside_other)):
            for first in range(0, width, 2 * TILE):
                last = min(first + 2 * TILE, width)
                value = jnp.dot(near[...], right[stream, :, first:last], preferred_element_type=jnp.float32)
                value += jnp.dot(far[...], right[1 - stream, :, first:last], preferred_element_type=jnp.float32)
                value = value.astype(jnp.bfloat16)
                for quarter in range(4):
                    rows = value[quarter * band : (quarter + 1) * band]
                    both[quarter % 2, side, quarter // 2, :, first:last] = rows
        keep[...] = both[odd]
        give[...] = both[1 - odd]

    vmem = pl.BlockSpec(memory_space=pltpu.VMEM)
    operands = [*blocks, *tiles[0], *tiles[1]]
    half = (2, 2, band, width)
    return pl.pallas_call(
        body,
        in_specs=[vmem] * len(operands),
        out_specs=[vmem, vmem],
        out_shape=[pltpu.VMEM(half, jnp.bfloat16)] * 2,
        scratch_shapes=[pltpu.VMEM((2, kloc, width), jnp.bfloat16), pltpu.VMEM((2, *half), jnp.bfloat16)],
        compiler_params=pltpu.CompilerParams(vmem_limit_bytes=KERNEL_VMEM),
        name="multiply",
    )(*[pltpu.with_memory_space_constraint(o, pltpu.VMEM) for o in operands])


def join(kept, came):
    width = sum(k.shape[-1] for k in kept)
    lead = kept[0].shape[:-1]

    def body(*refs):
        out = refs[-1]
        start = 0
        for mine, other in zip(refs[: len(kept)], refs[len(kept) : -1]):
            last = start + mine.shape[-1]
            total = mine[...].astype(jnp.float32) + other[...].astype(jnp.float32)
            out[:, :, :, start:last] = total.astype(jnp.bfloat16)
            start = last

    vmem = pl.BlockSpec(memory_space=pltpu.VMEM)
    return pl.pallas_call(
        body,
        in_specs=[vmem] * (2 * len(kept)),
        out_specs=vmem,
        out_shape=pltpu.VMEM((*lead, width), jnp.bfloat16),
        compiler_params=pltpu.CompilerParams(vmem_limit_bytes=KERNEL_VMEM),
        name="join",
    )(*[pltpu.with_memory_space_constraint(o, pltpu.VMEM) for o in (*kept, *came)])


def make(nz, ncol):
    every = ("z", "core", "yh", "yp", "x")
    nslot = nz // 2
    assert sum(CALLS) == nslot

    def on_device(amplitudes, integrals, amp_occupancy, int_occupancy, owner_map):
        z = lax.axis_index("z")
        own_tile = masked_tile(integrals, int_occupancy)
        nrow, _ = amplitudes.shape
        part = nrow // ncol
        current = [own_tile, own_tile]
        kept, came = [], []
        tiles = [[], []]
        for slot in range(1, nslot + 1):
            for stream in (0, 1):
                pairs = first_pairs(nz, ncol, stream) if slot == 1 else ring_pairs(nz, ncol)
                current[stream] = lax.ppermute(current[stream], every, pairs)
                tiles[stream].append(current[stream])
            if slot == 1:
                own = mask_tiles(amplitudes, amp_occupancy)
                beside = lax.ppermute(own, every, swap_pairs(nz, ncol, 0, 1))
                own_other = lax.ppermute(own, every, swap_pairs(nz, ncol, 1, 0))
                beside_other = lax.ppermute(beside, every, swap_pairs(nz, ncol, 1, 0))
                blocks = (own, beside, own_other, beside_other)
            call = len(kept)
            if slot == sum(CALLS[: call + 1]):
                keep, give = multiply(blocks, tiles)
                tiles = [[], []]
                came.append(lax.ppermute(give, every, swap_pairs(nz, ncol, 0, NX)))
                kept.append(keep)
        moved = join(kept, came).reshape(ncol, part, nslot * TILE)
        moved = lax.all_to_all(moved, ("core", "yh", "x"), 0, 0, tiled=True)
        moved = moved.reshape(2, ncol // 4, 2, part, nslot * TILE)
        done = jnp.sum(moved.astype(jnp.float32), 1).astype(jnp.bfloat16).reshape(4, part, nslot, TILE)
        done = done.transpose(0, 2, 1, 3).reshape(4 * nslot, part, TILE)
        chip = owner_map // 2
        parity = owner_map % 2
        behind = (z - chip) % nz
        upward = (behind >= 1) & (behind <= nslot)
        side = jnp.where(upward, 0, 2)
        slot_of = jnp.where(upward, behind - 1, (chip - z) % nz)
        place = (side + parity) * nslot + slot_of
        picked = done[place].reshape(ncol, 2, part, TILE).transpose(0, 2, 1, 3).reshape(ncol, part, 2 * TILE)
        final = lax.all_to_all(picked, every[2:], 0, 0, tiled=True)
        return final.reshape(nrow, 2 * TILE)

    return on_device


def solution(mesh):
    nz = mesh.shape["row"] // 2
    ncol = mesh.shape["col"]
    ny = ncol // NX
    fine = Mesh(mesh.devices.reshape(nz, 2, ny // 2, 2, NX), ("z", "core", "yh", "yp", "x"))
    split, col = ("z", "core"), ("yh", "yp", "x")
    placed = (P(split, col), P(col, split), P(split, col), P(col, split), P())
    return jax.shard_map(
        make(nz, ncol), mesh=fine, in_specs=placed, out_specs=P(split, col), check_vma=False
    )
```

```python
import jax
import jax.numpy as jnp
from jax import lax
from jax.experimental import pallas as pl
from jax.experimental.pallas import tpu as pltpu
from jax.sharding import Mesh, PartitionSpec as P


TILE = 128
KERNEL_VMEM = 16 << 20
NX = 4


def mask_tiles(matrix, occupancy):
    nrow, ncolumn = matrix.shape
    blocks = matrix.reshape(nrow // TILE, TILE, ncolumn // TILE, TILE)
    return (blocks * occupancy[:, None, :, None].astype(jnp.bfloat16)).reshape(nrow, ncolumn)


def rank(nz, ncol, z, core, col):
    return ((z % nz) * 2 + core) * ncol + col


def ring_pairs(nz, ncol):
    pairs = []
    for z in range(nz):
        for col in range(ncol):
            pairs.append((rank(nz, ncol, z, 0, col), rank(nz, ncol, z + 1, 0, col)))
            pairs.append((rank(nz, ncol, z, 1, col), rank(nz, ncol, z - 1, 1, col)))
    return pairs


def first_pairs(nz, ncol, far, flip):
    pairs = []
    for z in range(nz):
        for col in range(ncol):
            xp, yp = col & 1, col // NX & 1
            for core in (0, 1):
                home = (col & ~1 & ~NX) | (core ^ flip) | (yp ^ far) * NX
                source = rank(nz, ncol, z, xp, home)
                pairs.append((source, rank(nz, ncol, z + 1 if core == 0 else z, core, col)))
    return pairs


def swap_pairs(nz, ncol, core, col):
    return [
        (rank(nz, ncol, z, c, x), rank(nz, ncol, z, c ^ core, x ^ col))
        for z in range(nz) for c in (0, 1) for x in range(ncol)
    ]


def in_vmem(body, operands, scalars, out_shapes, scratch, aliases):
    vmem = pl.BlockSpec(memory_space=pltpu.VMEM)
    smem = pl.BlockSpec(memory_space=pltpu.SMEM)
    held = [pltpu.with_memory_space_constraint(o, pltpu.VMEM) for o in operands]
    return pl.pallas_call(
        body,
        in_specs=[smem] * len(scalars) + [vmem] * len(held),
        out_specs=[vmem] * len(out_shapes),
        out_shape=[pltpu.VMEM(shape, jnp.bfloat16) for shape in out_shapes],
        scratch_shapes=scratch,
        input_output_aliases=aliases,
        compiler_params=pltpu.CompilerParams(vmem_limit_bytes=KERNEL_VMEM),
    )(*scalars, *held)


def masked_halves(integrals, occupancy):
    kloc = integrals.shape[0]
    half = TILE // 2

    def body(occ, tile, near, far, both):
        for k in range(kloc // TILE):
            rows = slice(k * TILE, (k + 1) * TILE)
            block = (tile[rows, :].astype(jnp.float32) * occ[k].astype(jnp.float32)).T.astype(jnp.bfloat16)
            both[0, :, rows] = block[:half]
            both[1, :, rows] = block[half:]
        odd = lax.axis_index("yp")
        near[...] = both[odd]
        far[...] = both[1 - odd]

    return in_vmem(
        body, [integrals], [occupancy.reshape(-1)], [(half, kloc)] * 2,
        [pltpu.VMEM((2, half, kloc), jnp.bfloat16)], {},
    )


def multiply(blocks, tiles, start, width, previous):
    nrow, kloc = blocks[0][0].shape
    count = len(tiles[0])
    half = TILE // 2
    part = count * half

    def body(*refs):
        lefts, tile_refs = refs[:8], refs[8 : 8 + 2 * count]
        out, right = refs[-2:]
        core = lax.axis_index("core")
        flip = (lax.axis_index("xp") + core) % 2
        for i in range(2 * count):
            for upper in (0, 1):
                rows = slice(i % count * half, (i % count + 1) * half)
                right[2 * (i // count) + upper, rows, :] = tile_refs[i][upper * half : (upper + 1) * half, :]
        for side in (0, 1):
            total = None
            for far in (0, 1):
                for beside in (0, 1):
                    at = 2 * far + (flip if beside == 0 else 1 - flip)
                    value = lax.dot_general(
                        lefts[4 * side + 2 * far + beside][...], right[at],
                        (((1,), (1,)), ((), ())), preferred_element_type=jnp.float32,
                    )
                    total = value if total is None else total + value
            rows = core if side == 0 else 1 - core
            out[rows, :, start : start + part] = total.astype(jnp.bfloat16)

    operands = [*blocks[0], *blocks[1], *tiles[0], *tiles[1]]
    aliases = {}
    if previous is not None:
        aliases = {len(operands): 0}
        operands.append(previous)
    return in_vmem(body, operands, [], [(2, nrow, width)], [pltpu.VMEM((4, part, kloc), jnp.bfloat16)], aliases)[0]


def gather_tiles(moved, owner_map, nz, nslot):
    part = moved.shape[1]
    half = TILE // 2
    ntile = owner_map.shape[0]

    def body(owner, parts, out, done):
        low = lax.broadcasted_iota(jnp.int32, (part, TILE), 1) < half
        for core in (0, 1):
            for xp in (0, 1):
                for pair in range(nslot // 2):
                    cols = slice(pair * TILE, (pair + 1) * TILE)
                    sums = []
                    for yp in (0, 1):
                        total = None
                        for yh in (0, 1):
                            for xh in (0, 1):
                                at = core * 16 + yh * 8 + yp * 4 + xh * 2 + xp
                                value = parts[at, :, cols].astype(jnp.float32)
                                total = value if total is None else total + value
                        sums.append(total)
                    first = jnp.where(low, sums[0], pltpu.roll(sums[1], half, 1))
                    second = jnp.where(low, pltpu.roll(sums[0], half, 1), sums[1])
                    base = (core * 2 + xp) * nslot + 2 * pair
                    done[base] = first.astype(jnp.bfloat16)
                    done[base + 1] = second.astype(jnp.bfloat16)
        z = lax.axis_index("z")
        for t in range(ntile):
            tile = owner[t]
            chip = tile // 2
            behind = (z - chip + nz) % nz
            upward = (behind >= 1) & (behind <= nslot)
            place = jnp.where(upward, behind - 1, 2 * nslot + (chip - z + nz) % nz) + tile % 2 * nslot
            out[t // 2, :, t % 2 * TILE : (t % 2 + 1) * TILE] = done[place]

    return in_vmem(
        body, [moved], [owner_map], [(ntile // 2, part, 2 * TILE)],
        [pltpu.VMEM((4 * nslot, part, TILE), jnp.bfloat16)], {},
    )[0]


CALLS = (8,)


def make(nz, ncol):
    cols = ("yh", "yp", "xh", "xp")
    every = ("z", "core", *cols)
    nslot = nz // 2

    def on_device(amplitudes, integrals, amp_occupancy, int_occupancy, owner_map):
        nrow = amplitudes.shape[0]
        part = nrow // ncol
        half = TILE // 2
        near, far = masked_halves(integrals, int_occupancy)
        pieces = []
        for j in range(4):
            pairs = first_pairs(nz, ncol, j // 2, j % 2)
            pieces.append(lax.ppermute(far if j // 2 else near, every, pairs))
        current = [jnp.concatenate(pieces[:2], 0), jnp.concatenate(pieces[2:], 0)]
        own = mask_tiles(amplitudes, amp_occupancy)
        blocks = [[own], []]
        for col in (1, NX, NX + 1):
            blocks[0].append(lax.ppermute(own, every, swap_pairs(nz, ncol, 0, col)))
        for block in blocks[0]:
            blocks[1].append(lax.ppermute(block, every, swap_pairs(nz, ncol, 1, 0)))
        tiles = [[current[0]], [current[1]]]
        product = None
        call = 0
        begin = 0
        for slot in range(2, nslot + 1):
            for stream in (0, 1):
                current[stream] = lax.ppermute(current[stream], every, ring_pairs(nz, ncol))
                tiles[stream].append(current[stream])
            if slot == begin + CALLS[call]:
                product = multiply(blocks, tiles, begin * half, nslot * half, product)
                tiles = [[], []]
                begin = slot
                call += 1
        product = product.reshape(2 * ncol, part, nslot * half)
        moved = lax.all_to_all(product, every[1:], 0, 0, tiled=True)
        picked = gather_tiles(moved, owner_map, nz, nslot)
        final = lax.all_to_all(picked, cols, 0, 0, tiled=True)
        return final.reshape(nrow, 2 * TILE)

    return on_device


def solution(mesh):
    nz = mesh.shape["row"] // 2
    ncol = mesh.shape["col"]
    ny = ncol // NX
    shape = (nz, 2, ny // 2, 2, NX // 2, 2)
    fine = Mesh(mesh.devices.reshape(shape), ("z", "core", "yh", "yp", "xh", "xp"))
    split, col = ("z", "core"), ("yh", "yp", "xh", "xp")
    placed = (P(split, col), P(col, split), P(split, col), P(col, split), P())
    return jax.shard_map(
        make(nz, ncol), mesh=fine, in_specs=placed, out_specs=P(split, col), check_vma=False
    )
```

```python
import jax
import jax.numpy as jnp
from jax import lax
from jax.experimental import pallas as pl
from jax.experimental.pallas import tpu as pltpu
from jax.sharding import Mesh, PartitionSpec as P


TILE = 128
KERNEL_VMEM = 16 << 20


def mask_tiles(matrix, occupancy):
    nrow, ncolumn = matrix.shape
    blocks = matrix.reshape(nrow // TILE, TILE, ncolumn // TILE, TILE)
    return (blocks * occupancy[:, None, :, None].astype(jnp.bfloat16)).reshape(nrow, ncolumn)


def rank(nz, ncol, z, core, col):
    return ((z % nz) * 2 + core) * ncol + col


def ring_pairs(nz, ncol):
    pairs = []
    for z in range(nz):
        for col in range(ncol):
            pairs.append((rank(nz, ncol, z, 0, col), rank(nz, ncol, z + 1, 0, col)))
            pairs.append((rank(nz, ncol, z, 1, col), rank(nz, ncol, z - 1, 1, col)))
    return pairs


def first_pairs(nz, ncol, stream):
    pairs = []
    for z in range(nz):
        for col in range(ncol):
            even = col & ~1
            for core in (0, 1):
                source = rank(nz, ncol, z, col & 1, even | (core ^ stream))
                target = rank(nz, ncol, z + 1 if core == 0 else z, core, col)
                pairs.append((source, target))
    return pairs


def swap_pairs(nz, ncol, core, col):
    return [
        (rank(nz, ncol, z, c, x), rank(nz, ncol, z, c ^ core, x ^ col))
        for z in range(nz) for c in (0, 1) for x in range(ncol)
    ]


CHUNKS = ((4,), (4,))


def calls_of():
    calls = []
    slot = 0
    for k, chunk in enumerate(CHUNKS):
        begin = 0
        for count in chunk:
            slot += count
            calls.append((slot, k, count, begin, sum(chunk)))
            begin += count
    return calls


def masked_tile(integrals, occupancy):
    def body(occ, tile, out):
        for k in range(tile.shape[0] // TILE):
            rows = slice(k * TILE, (k + 1) * TILE)
            out[rows, :] = tile[rows, :] * occ[k].astype(jnp.float32).astype(jnp.bfloat16)

    return pl.pallas_call(
        body,
        in_specs=[pl.BlockSpec(memory_space=pltpu.SMEM), pl.BlockSpec(memory_space=pltpu.VMEM)],
        out_specs=pl.BlockSpec(memory_space=pltpu.VMEM),
        out_shape=pltpu.VMEM(integrals.shape, jnp.bfloat16),
        compiler_params=pltpu.CompilerParams(vmem_limit_bytes=KERNEL_VMEM),
        name="masked_tile",
    )(occupancy.reshape(-1), integrals)


def multiply(blocks, tiles, start, width, previous):
    nrow, kloc = blocks[0].shape
    count = len(tiles[0])
    part = count * TILE

    def body(own, beside, own_other, beside_other, *rest):
        tile_refs = rest[: 2 * count]
        out, right = rest[-2:]
        core = lax.axis_index("core")
        stream = (lax.axis_index("col") + core) % 2
        for i in range(2 * count):
            right[i // count, :, (i % count) * TILE : (i % count + 1) * TILE] = tile_refs[i][...]
        for side, near, far in ((core, own, beside), (1 - core, own_other, beside_other)):
            for first in range(0, part, 2 * TILE):
                last = min(first + 2 * TILE, part)
                value = jnp.dot(near[...], right[stream, :, first:last], preferred_element_type=jnp.float32)
                value += jnp.dot(far[...], right[1 - stream, :, first:last], preferred_element_type=jnp.float32)
                out[side, :, start + first : start + last] = value.astype(jnp.bfloat16)

    vmem = pl.BlockSpec(memory_space=pltpu.VMEM)
    operands = [*blocks, *tiles[0], *tiles[1]]
    aliases = {}
    if previous is not None:
        aliases = {len(operands): 0}
        operands.append(previous)
    return pl.pallas_call(
        body,
        in_specs=[vmem] * len(operands),
        out_specs=vmem,
        out_shape=pltpu.VMEM((2, nrow, width), jnp.bfloat16),
        scratch_shapes=[pltpu.VMEM((2, kloc, part), jnp.bfloat16)],
        input_output_aliases=aliases,
        compiler_params=pltpu.CompilerParams(vmem_limit_bytes=KERNEL_VMEM),
        name="multiply",
    )(*[pltpu.with_memory_space_constraint(o, pltpu.VMEM) for o in operands])


def gather_tiles(early, late, owner_map, nz, nslot):
    part = late.shape[1]
    ntile = owner_map.shape[0]
    ncol = late.shape[0] // 2

    def body(owner, summed, parts, out, done):
        before = summed.shape[-1] // TILE
        for core in (0, 1):
            for odd in (0, 1):
                base = (core * 2 + odd) * nslot
                for slot in range(before):
                    done[base + slot] = summed[core * 2 + odd, :, slot * TILE : (slot + 1) * TILE]
                for slot in range(before, nslot):
                    cols = slice((slot - before) * TILE, (slot - before + 1) * TILE)
                    total = None
                    for col in range(odd, ncol, 2):
                        value = parts[core * ncol + col, :, cols].astype(jnp.float32)
                        total = value if total is None else total + value
                    done[base + slot] = total.astype(jnp.bfloat16)
        z = lax.axis_index("z")
        for t in range(ntile):
            tile = owner[t]
            chip = tile // 2
            behind = (z - chip + nz) % nz
            upward = (behind >= 1) & (behind <= nslot)
            place = jnp.where(upward, behind - 1, 2 * nslot + (chip - z + nz) % nz) + tile % 2 * nslot
            out[t // 2, :, t % 2 * TILE : (t % 2 + 1) * TILE] = done[place]

    vmem = pl.BlockSpec(memory_space=pltpu.VMEM)
    return pl.pallas_call(
        body,
        in_specs=[pl.BlockSpec(memory_space=pltpu.SMEM), vmem, vmem],
        out_specs=vmem,
        out_shape=pltpu.VMEM((ntile // 2, part, 2 * TILE), jnp.bfloat16),
        scratch_shapes=[pltpu.VMEM((4 * nslot, part, TILE), jnp.bfloat16)],
        compiler_params=pltpu.CompilerParams(vmem_limit_bytes=KERNEL_VMEM),
        name="gather_tiles",
    )(owner_map, *[pltpu.with_memory_space_constraint(o, pltpu.VMEM) for o in (early, late)])


def make(nz, ncol):
    every = ("z", "core", "col")
    nslot = nz // 2
    assert sum(map(sum, CHUNKS)) == nslot

    def on_device(amplitudes, integrals, amp_occupancy, int_occupancy, owner_map):
        own_tile = masked_tile(integrals, int_occupancy)
        nrow, _ = amplitudes.shape
        part = nrow // ncol
        current = [own_tile, own_tile]
        sums = []
        tiles = [[], []]
        ends = calls_of()
        call = 0
        product = None
        for slot in range(1, nslot + 1):
            for stream in (0, 1):
                pairs = first_pairs(nz, ncol, stream) if slot == 1 else ring_pairs(nz, ncol)
                current[stream] = lax.ppermute(current[stream], every, pairs)
                tiles[stream].append(current[stream])
            if slot == 1:
                own = mask_tiles(amplitudes, amp_occupancy)
                beside = lax.ppermute(own, every, swap_pairs(nz, ncol, 0, 1))
                own_other = lax.ppermute(own, every, swap_pairs(nz, ncol, 1, 0))
                beside_other = lax.ppermute(beside, every, swap_pairs(nz, ncol, 1, 0))
                blocks = (own, beside, own_other, beside_other)
            if slot == ends[call][0]:
                _, _, count, begin, width = ends[call]
                product = multiply(blocks, tiles, begin * TILE, width * TILE, product)
                tiles = [[], []]
                call += 1
                if begin + count < width:
                    continue
                width = product.shape[-1]
                moved = product.reshape(2 * ncol, part, width)
                product = None
                moved = lax.all_to_all(moved, ("core", "col"), 0, 0, tiled=True)
                sums.append(moved)
        early = sums[0].reshape(2, ncol // 2, 2, part, -1)
        early = jnp.sum(early.astype(jnp.float32), 1).astype(jnp.bfloat16).reshape(4, part, -1)
        picked = gather_tiles(early, sums[1], owner_map, nz, nslot)
        final = lax.all_to_all(picked, "col", 0, 0, tiled=True)
        return final.reshape(nrow, 2 * TILE)

    return on_device


def solution(mesh):
    nz = mesh.shape["row"] // 2
    ncol = mesh.shape["col"]
    fine = Mesh(mesh.devices.reshape(nz, 2, ncol), ("z", "core", "col"))
    split = ("z", "core")
    placed = (P(split, "col"), P("col", split), P(split, "col"), P("col", split), P())
    return jax.shard_map(
        make(nz, ncol), mesh=fine, in_specs=placed, out_specs=P(split, "col"), check_vma=False
    )
```

```python
import jax
import jax.numpy as jnp
from jax import lax
from jax.experimental import pallas as pl
from jax.experimental.pallas import tpu as pltpu
from jax.sharding import Mesh, PartitionSpec as P


TILE = 128
KERNEL_VMEM = 16 << 20


def mask_tiles(matrix, occupancy):
    nrow, ncolumn = matrix.shape
    blocks = matrix.reshape(nrow // TILE, TILE, ncolumn // TILE, TILE)
    return (blocks * occupancy[:, None, :, None].astype(jnp.bfloat16)).reshape(nrow, ncolumn)


def rank(nz, ncol, z, core, col):
    return ((z % nz) * 2 + core) * ncol + col


def ring_pairs(nz, ncol):
    pairs = []
    for z in range(nz):
        for col in range(ncol):
            pairs.append((rank(nz, ncol, z, 0, col), rank(nz, ncol, z + 1, 0, col)))
            pairs.append((rank(nz, ncol, z, 1, col), rank(nz, ncol, z - 1, 1, col)))
    return pairs


def first_pairs(nz, ncol, stream):
    pairs = []
    for z in range(nz):
        for col in range(ncol):
            even = col & ~1
            for core in (0, 1):
                source = rank(nz, ncol, z, col & 1, even | (core ^ stream))
                pairs.append((source, rank(nz, ncol, z + 1 - 2 * core, core, col)))
    return pairs


def own_pairs(nz, ncol):
    return [
        (rank(nz, ncol, z, col & 1, (col & ~1) | core), rank(nz, ncol, z, core, col))
        for z in range(nz) for col in range(ncol) for core in (0, 1)
    ]


def swap_pairs(nz, ncol, core, col):
    return [
        (rank(nz, ncol, z, c, x), rank(nz, ncol, z, c ^ core, x ^ col))
        for z in range(nz) for c in (0, 1) for x in range(ncol)
    ]


CHUNKS = ((5,), (3, 1))


def calls_of():
    calls = []
    slot = -1
    for k, chunk in enumerate(CHUNKS):
        begin = 0
        for count in chunk:
            slot += count
            calls.append((slot, k, count, begin, sum(chunk)))
            begin += count
    return calls


def masked_tile(integrals, occupancy):
    def body(occ, tile, out):
        for k in range(tile.shape[0] // TILE):
            rows = slice(k * TILE, (k + 1) * TILE)
            out[rows, :] = tile[rows, :] * occ[k].astype(jnp.float32).astype(jnp.bfloat16)

    return pl.pallas_call(
        body,
        in_specs=[pl.BlockSpec(memory_space=pltpu.SMEM), pl.BlockSpec(memory_space=pltpu.VMEM)],
        out_specs=pl.BlockSpec(memory_space=pltpu.VMEM),
        out_shape=pltpu.VMEM(integrals.shape, jnp.bfloat16),
        compiler_params=pltpu.CompilerParams(vmem_limit_bytes=KERNEL_VMEM),
        name="masked_tile",
    )(occupancy.reshape(-1), integrals)


def multiply(blocks, tiles, start, width, previous):
    nrow, kloc = blocks[0].shape
    count = len(tiles[0])
    part = count * TILE

    def body(own, beside, own_other, beside_other, *rest):
        out, right = rest[-2:]
        core = lax.axis_index("core")
        stream = (lax.axis_index("col") + core) % 2
        used = 0
        for i in range(2 * count):
            cols = slice((i % count) * TILE, (i % count + 1) * TILE)
            if tiles[i // count][i % count] is None:
                right[i // count, :, cols] = jnp.zeros((kloc, TILE), jnp.bfloat16)
            else:
                right[i // count, :, cols] = rest[used][...]
                used += 1
        for side, near, far in ((core, own, beside), (1 - core, own_other, beside_other)):
            if all(t is None for t in tiles[1]):
                for pick, left in ((0, near), (1, far)):

                    @pl.when(stream == pick)
                    def _(side=side, left=left):
                        value = jnp.dot(left[...], right[0], preferred_element_type=jnp.float32)
                        out[side, :, start : start + part] = value.astype(jnp.bfloat16)

                continue
            for first in range(0, part, 2 * TILE):
                last = min(first + 2 * TILE, part)
                value = jnp.dot(near[...], right[stream, :, first:last], preferred_element_type=jnp.float32)
                value += jnp.dot(far[...], right[1 - stream, :, first:last], preferred_element_type=jnp.float32)
                out[side, :, start + first : start + last] = value.astype(jnp.bfloat16)

    vmem = pl.BlockSpec(memory_space=pltpu.VMEM)
    operands = [*blocks, *(t for t in tiles[0] + tiles[1] if t is not None)]
    aliases = {}
    if previous is not None:
        aliases = {len(operands): 0}
        operands.append(previous)
    return pl.pallas_call(
        body,
        in_specs=[vmem] * len(operands),
        out_specs=vmem,
        out_shape=pltpu.VMEM((2, nrow, width), jnp.bfloat16),
        scratch_shapes=[pltpu.VMEM((2, kloc, part), jnp.bfloat16)],
        input_output_aliases=aliases,
        compiler_params=pltpu.CompilerParams(vmem_limit_bytes=KERNEL_VMEM),
        name="multiply",
    )(*[pltpu.with_memory_space_constraint(o, pltpu.VMEM) for o in operands])


def gather_tiles(early, late, owner_map, nz, nslot):
    part = late.shape[1]
    ntile = owner_map.shape[0]
    ncol = late.shape[0] // 2

    before = early.shape[-1] // TILE
    block = nslot + 1

    def body(owner, first, second, out, done):
        def total_of(core, odd, slot):
            parts, at = (first, slot) if slot < before else (second, slot - before)
            total = None
            for col in range(odd, ncol, 2):
                value = parts[core * ncol + col, :, at * TILE : (at + 1) * TILE].astype(jnp.float32)
                total = value if total is None else total + value
            return total

        for odd in (0, 1):
            for slot in range(block):
                if slot in (0, nslot):
                    both = total_of(0, odd, slot) + total_of(1, odd, slot)
                    done[odd * block + slot] = both.astype(jnp.bfloat16)
                    continue
                for core in (0, 1):
                    done[(core * 2 + odd) * block + slot] = total_of(core, odd, slot).astype(jnp.bfloat16)
        z = lax.axis_index("z")
        for t in range(ntile):
            tile = owner[t]
            chip = tile // 2
            behind = (z - chip + nz) % nz
            place = jnp.where(behind <= nslot, behind, 2 * block + nz - behind) + tile % 2 * block
            out[t // 2, :, t % 2 * TILE : (t % 2 + 1) * TILE] = done[place]

    vmem = pl.BlockSpec(memory_space=pltpu.VMEM)
    return pl.pallas_call(
        body,
        in_specs=[pl.BlockSpec(memory_space=pltpu.SMEM), vmem, vmem],
        out_specs=vmem,
        out_shape=pltpu.VMEM((ntile // 2, part, 2 * TILE), jnp.bfloat16),
        scratch_shapes=[pltpu.VMEM((4 * (nslot + 1), part, TILE), jnp.bfloat16)],
        compiler_params=pltpu.CompilerParams(vmem_limit_bytes=KERNEL_VMEM),
        name="gather_tiles",
    )(owner_map, *[pltpu.with_memory_space_constraint(o, pltpu.VMEM) for o in (early, late)])


def make(nz, ncol):
    every = ("z", "core", "col")
    nslot = nz // 2
    assert sum(map(sum, CHUNKS)) == nslot + 1

    def on_device(amplitudes, integrals, amp_occupancy, int_occupancy, owner_map):
        own_tile = masked_tile(integrals, int_occupancy)
        nrow, _ = amplitudes.shape
        part = nrow // ncol
        current = [own_tile, own_tile]
        sums = []
        tiles = [[lax.ppermute(own_tile, every, own_pairs(nz, ncol))], [None]]
        ends = calls_of()
        call = 0
        product = None
        for slot in range(1, nslot + 1):
            for stream in (0, 1):
                if stream == 1 and slot == nslot:
                    tiles[1].append(None)
                    continue
                pairs = first_pairs(nz, ncol, stream) if slot == 1 else ring_pairs(nz, ncol)
                current[stream] = lax.ppermute(current[stream], every, pairs)
                tiles[stream].append(current[stream])
            if slot == 1:
                own = mask_tiles(amplitudes, amp_occupancy)
                beside = lax.ppermute(own, every, swap_pairs(nz, ncol, 0, 1))
                own_other = lax.ppermute(own, every, swap_pairs(nz, ncol, 1, 0))
                beside_other = lax.ppermute(beside, every, swap_pairs(nz, ncol, 1, 0))
                blocks = (own, beside, own_other, beside_other)
            if slot == ends[call][0]:
                _, _, count, begin, width = ends[call]
                product = multiply(blocks, tiles, begin * TILE, width * TILE, product)
                tiles = [[], []]
                call += 1
                if begin + count < width:
                    continue
                width = product.shape[-1]
                moved = product.reshape(2 * ncol, part, width)
                product = None
                moved = lax.all_to_all(moved, ("core", "col"), 0, 0, tiled=True)
                sums.append(moved)
        picked = gather_tiles(sums[0], sums[1], owner_map, nz, nslot)
        final = lax.all_to_all(picked, "col", 0, 0, tiled=True)
        return final.reshape(nrow, 2 * TILE)

    return on_device


def solution(mesh):
    nz = mesh.shape["row"] // 2
    ncol = mesh.shape["col"]
    fine = Mesh(mesh.devices.reshape(nz, 2, ncol), ("z", "core", "col"))
    split = ("z", "core")
    placed = (P(split, "col"), P("col", split), P(split, "col"), P("col", split), P())
    return jax.shard_map(
        make(nz, ncol), mesh=fine, in_specs=placed, out_specs=P(split, "col"), check_vma=False
    )
```

```python
import jax
import jax.numpy as jnp
from jax import lax
from jax.experimental import pallas as pl
from jax.experimental.pallas import tpu as pltpu
from jax.sharding import Mesh, PartitionSpec as P


TILE = 128
KERNEL_VMEM = 16 << 20


def mask_tiles(matrix, occupancy):
    nrow, ncolumn = matrix.shape
    blocks = matrix.reshape(nrow // TILE, TILE, ncolumn // TILE, TILE)
    return (blocks * occupancy[:, None, :, None].astype(jnp.bfloat16)).reshape(nrow, ncolumn)


def rank(nz, ncol, z, core, col):
    return ((z % nz) * 2 + core) * ncol + col


def ring_pairs(nz, ncol):
    pairs = []
    for z in range(nz):
        for col in range(ncol):
            pairs.append((rank(nz, ncol, z, 0, col), rank(nz, ncol, z + 1, 0, col)))
            pairs.append((rank(nz, ncol, z, 1, col), rank(nz, ncol, z - 1, 1, col)))
    return pairs


def first_pairs(nz, ncol, stream):
    pairs = []
    for z in range(nz):
        for col in range(ncol):
            even = col & ~1
            for core in (0, 1):
                source = rank(nz, ncol, z, col & 1, even | (core ^ stream))
                pairs.append((source, rank(nz, ncol, z + 1 - 2 * core, core, col)))
    return pairs


def own_pairs(nz, ncol):
    return [
        (rank(nz, ncol, z, col & 1, (col & ~1) | core), rank(nz, ncol, z, core, col))
        for z in range(nz) for col in range(ncol) for core in (0, 1)
    ]


def swap_pairs(nz, ncol, core, col):
    return [
        (rank(nz, ncol, z, c, x), rank(nz, ncol, z, c ^ core, x ^ col))
        for z in range(nz) for c in (0, 1) for x in range(ncol)
    ]


CHUNKS = ((6,), (2, 1))


def calls_of():
    calls = []
    slot = -1
    for k, chunk in enumerate(CHUNKS):
        begin = 0
        for count in chunk:
            slot += count
            calls.append((slot, k, count, begin, sum(chunk)))
            begin += count
    return calls


def masked_tile(integrals, occupancy):
    def body(occ, tile, out):
        for k in range(tile.shape[0] // TILE):
            rows = slice(k * TILE, (k + 1) * TILE)
            out[rows, :] = tile[rows, :] * occ[k].astype(jnp.float32).astype(jnp.bfloat16)

    return pl.pallas_call(
        body,
        in_specs=[pl.BlockSpec(memory_space=pltpu.SMEM), pl.BlockSpec(memory_space=pltpu.VMEM)],
        out_specs=pl.BlockSpec(memory_space=pltpu.VMEM),
        out_shape=pltpu.VMEM(integrals.shape, jnp.bfloat16),
        compiler_params=pltpu.CompilerParams(vmem_limit_bytes=KERNEL_VMEM),
        name="masked_tile",
    )(occupancy.reshape(-1), integrals)


def multiply(blocks, tiles, start, width, previous):
    nrow, kloc = blocks[0].shape
    count = len(tiles[0])
    part = count * TILE

    def body(own, beside, own_other, beside_other, *rest):
        out, right = rest[-2:]
        core = lax.axis_index("core")
        stream = (lax.axis_index("col") + core) % 2
        used = 0
        for i in range(2 * count):
            cols = slice((i % count) * TILE, (i % count + 1) * TILE)
            if tiles[i // count][i % count] is None:
                right[i // count, :, cols] = jnp.zeros((kloc, TILE), jnp.bfloat16)
            else:
                right[i // count, :, cols] = rest[used][...]
                used += 1
        for side, near, far in ((core, own, beside), (1 - core, own_other, beside_other)):
            for first in range(0, part, 2 * TILE):
                last = min(first + 2 * TILE, part)
                value = jnp.dot(near[...], right[stream, :, first:last], preferred_element_type=jnp.float32)
                value += jnp.dot(far[...], right[1 - stream, :, first:last], preferred_element_type=jnp.float32)
                out[side, :, start + first : start + last] = value.astype(jnp.bfloat16)

    vmem = pl.BlockSpec(memory_space=pltpu.VMEM)
    operands = [*blocks, *(t for t in tiles[0] + tiles[1] if t is not None)]
    aliases = {}
    if previous is not None:
        aliases = {len(operands): 0}
        operands.append(previous)
    return pl.pallas_call(
        body,
        in_specs=[vmem] * len(operands),
        out_specs=vmem,
        out_shape=pltpu.VMEM((2, nrow, width), jnp.bfloat16),
        scratch_shapes=[pltpu.VMEM((2, kloc, part), jnp.bfloat16)],
        input_output_aliases=aliases,
        compiler_params=pltpu.CompilerParams(vmem_limit_bytes=KERNEL_VMEM),
        name="multiply",
    )(*[pltpu.with_memory_space_constraint(o, pltpu.VMEM) for o in operands])


def gather_tiles(early, late, owner_map, nz, nslot):
    part = late.shape[1]
    ntile = owner_map.shape[0]
    ncol = late.shape[0] // 2

    def body(owner, summed, parts, out, done):
        before = summed.shape[-1] // TILE
        block = nslot + 1
        for odd in (0, 1):
            own = summed[odd, :, :TILE].astype(jnp.float32) + summed[2 + odd, :, :TILE].astype(jnp.float32)
            done[odd * block] = own.astype(jnp.bfloat16)
            half_way = None
            for core in (0, 1):
                base = (core * 2 + odd) * block
                for slot in range(1, before):
                    done[base + slot] = summed[core * 2 + odd, :, slot * TILE : (slot + 1) * TILE]
                for slot in range(before, nslot + 1):
                    cols = slice((slot - before) * TILE, (slot - before + 1) * TILE)
                    total = half_way if slot == nslot else None
                    for col in range(odd, ncol, 2):
                        value = parts[core * ncol + col, :, cols].astype(jnp.float32)
                        total = value if total is None else total + value
                    if slot == nslot:
                        half_way = total
                    else:
                        done[base + slot] = total.astype(jnp.bfloat16)
            done[odd * block + nslot] = half_way.astype(jnp.bfloat16)
        z = lax.axis_index("z")
        for t in range(ntile):
            tile = owner[t]
            chip = tile // 2
            behind = (z - chip + nz) % nz
            place = jnp.where(behind <= nslot, behind, 2 * block + nz - behind) + tile % 2 * block
            out[t // 2, :, t % 2 * TILE : (t % 2 + 1) * TILE] = done[place]

    vmem = pl.BlockSpec(memory_space=pltpu.VMEM)
    return pl.pallas_call(
        body,
        in_specs=[pl.BlockSpec(memory_space=pltpu.SMEM), vmem, vmem],
        out_specs=vmem,
        out_shape=pltpu.VMEM((ntile // 2, part, 2 * TILE), jnp.bfloat16),
        scratch_shapes=[pltpu.VMEM((4 * (nslot + 1), part, TILE), jnp.bfloat16)],
        compiler_params=pltpu.CompilerParams(vmem_limit_bytes=KERNEL_VMEM),
        name="gather_tiles",
    )(owner_map, *[pltpu.with_memory_space_constraint(o, pltpu.VMEM) for o in (early, late)])


def make(nz, ncol):
    every = ("z", "core", "col")
    nslot = nz // 2
    assert sum(map(sum, CHUNKS)) == nslot + 1

    def on_device(amplitudes, integrals, amp_occupancy, int_occupancy, owner_map):
        own_tile = masked_tile(integrals, int_occupancy)
        nrow, _ = amplitudes.shape
        part = nrow // ncol
        current = [own_tile, own_tile]
        sums = []
        tiles = [[lax.ppermute(own_tile, every, own_pairs(nz, ncol))], [None]]
        ends = calls_of()
        call = 0
        product = None
        for slot in range(1, nslot + 1):
            for stream in (0, 1):
                if stream == 1 and slot == nslot:
                    tiles[1].append(None)
                    continue
                pairs = first_pairs(nz, ncol, stream) if slot == 1 else ring_pairs(nz, ncol)
                current[stream] = lax.ppermute(current[stream], every, pairs)
                tiles[stream].append(current[stream])
            if slot == 1:
                own = mask_tiles(amplitudes, amp_occupancy)
                beside = lax.ppermute(own, every, swap_pairs(nz, ncol, 0, 1))
                own_other = lax.ppermute(own, every, swap_pairs(nz, ncol, 1, 0))
                beside_other = lax.ppermute(beside, every, swap_pairs(nz, ncol, 1, 0))
                blocks = (own, beside, own_other, beside_other)
            if slot == ends[call][0]:
                _, _, count, begin, width = ends[call]
                product = multiply(blocks, tiles, begin * TILE, width * TILE, product)
                tiles = [[], []]
                call += 1
                if begin + count < width:
                    continue
                width = product.shape[-1]
                moved = product.reshape(2 * ncol, part, width)
                product = None
                moved = lax.all_to_all(moved, ("core", "col"), 0, 0, tiled=True)
                sums.append(moved)
        early = sums[0].reshape(2, ncol // 2, 2, part, -1)
        early = jnp.sum(early.astype(jnp.float32), 1).astype(jnp.bfloat16).reshape(4, part, -1)
        picked = gather_tiles(early, sums[1], owner_map, nz, nslot)
        final = lax.all_to_all(picked, "col", 0, 0, tiled=True)
        return final.reshape(nrow, 2 * TILE)

    return on_device


def solution(mesh):
    nz = mesh.shape["row"] // 2
    ncol = mesh.shape["col"]
    fine = Mesh(mesh.devices.reshape(nz, 2, ncol), ("z", "core", "col"))
    split = ("z", "core")
    placed = (P(split, "col"), P("col", split), P(split, "col"), P("col", split), P())
    return jax.shard_map(
        make(nz, ncol), mesh=fine, in_specs=placed, out_specs=P(split, "col"), check_vma=False
    )
```
